256 devices in a mesh: member: 4 (over y, x), ty: 64 (over z, core).
Axes of the slice: x: 2, y: 2, z: 32, core: 2. Of those that a mesh axis runs over, the one named last changes fastest.
The devices are a block of a 4x8x32 slice.
Arguments:
- fields: float32 [64, 768, 6, 768], P('member', 'ty'), parts along dimension 0, may hold values from -6 to 6
- damp_four: float32 [64], P('member'), parts along dimension 0, may hold values from 0.004 to 0.03
- damp_six: float32 [64], P('member'), parts along dimension 0, may hold values from 0.0008 to 0.006
- metric: float32 [4, 768, 6, 768], P(None, 'ty'), may hold values from 0.1 to 1.9
- seam_table: int32 [6, 4, 3], replicated, may hold values from 0 to 5, as said below
Outputs:
- damped: float32 [64, 768, 6, 768], P('member', 'ty'), parts along dimension 0
The draws below stay inside these ranges and needn't reach their ends.
There are 4 independent parts, one for each index of `member`. The reference program is written for one: setup_inputs(seed, part) draws one part's arguments, and reference() takes and returns one part's arrays. A program takes and returns all parts, laid end to end along the dimension named above; an argument that names none is the same for every part. Nothing has to cross between parts.
Inputs may be any that keep to these rules, and one draw needn't show every extreme that they name: seam_table[f, e] = (g, h, r) joins edge e of face f (edge codes as in the reference program) to edge h of face g; r = 1 when the cells of the two edges run in opposite index order. The table describes the surface of a cube with every face seen from outside: the joining is symmetric, no face is joined to itself, and r is 1 exactly when both edges are among (south, east) or both among (north, west).
All inputs are finite; a program needn't handle non-finite values.
Results may differ from the reference program's by a relative error of at most 0.00005.
Values sent between devices are 32-bit elements; how exact they have to be, the bound alone decides.
A program may use at most 64 MiB of HBM per device.

```python
import math
import jax
import jax.numpy as jnp
import numpy as np

C = 768
FACES = 6
LEV = 16


def vector_cross(first, second):
    return (first[1] * second[2] - first[2] * second[1], first[2] * second[0] - first[0] * second[2], first[0] * second[1] - first[1] * second[0])


def negated(vector):
    return (-vector[0], -vector[1], -vector[2])


def cube_table():
    normals = [(1, 0, 0), (-1, 0, 0), (0, 1, 0), (0, -1, 0), (0, 0, 1), (0, 0, -1)]
    tangents = [(0, 1, 0), (0, 0, 1), (0, 0, 1), (1, 0, 0), (1, 0, 0), (0, 1, 0)]
    outward = []
    for face in range(6):
        along = tangents[face]
        upward = vector_cross(normals[face], along)
        outward.append([negated(upward), along, upward, negated(along)])
    result = np.zeros((6, 4, 2), np.int64)
    for face in range(6):
        for side in range(4):
            other = [g for g in range(6) if normals[g] == outward[face][side]][0]
            other_side = [h for h in range(4) if outward[other][h] == normals[face]][0]
            result[face, side, 0] = other
            result[face, side, 1] = other_side
    return result


def draw_seam_table(key, part):
    joined = cube_table()
    first_key, second_key = jax.random.split(jax.random.fold_in(key, 7))
    relabel = jax.random.permutation(first_key, 6).astype(jnp.int32)
    rotation = jax.random.randint(second_key, (6,), 0, 4).astype(jnp.int32)
    face_ids = np.repeat(np.arange(6), 4)
    side_ids = np.tile(np.arange(4), 6)
    other_face = joined[:, :, 0].reshape(-1)
    other_side = joined[:, :, 1].reshape(-1)
    new_face = relabel[face_ids]
    new_side = (jnp.asarray(side_ids, jnp.int32) + rotation[face_ids]) % 4
    near_face = relabel[other_face]
    near_side = (jnp.asarray(other_side, jnp.int32) + rotation[other_face]) % 4
    flipped = ((new_side < 2) == (near_side < 2)).astype(jnp.int32)
    entries = jnp.stack([near_face, near_side, flipped], axis=-1).astype(jnp.int32)
    return jnp.zeros((6, 4, 3), jnp.int32).at[new_face, new_side].set(entries)


def level_of(key, dims, pieces, low, high):
    def one(position, blocks):
        steps = jax.random.uniform(jax.random.fold_in(jax.random.fold_in(key, 6), position), (blocks,), jnp.float32, low / len(pieces), high / len(pieces))
        return jnp.repeat(jnp.exp(steps), dims[position] // blocks).reshape((-1,) + (1,) * (len(dims) - position - 1))

    gain = one(*pieces[0])
    for cut in pieces[1:]:
        gain = gain * one(*cut)
    return gain


def centred(key, shape, scale, bound, cuts=(), held_as=jnp.bfloat16):
    values = jax.random.normal(key, shape, jnp.float32) * scale
    if len(cuts) > 0:
        values = level_of(key, shape, cuts, -0.22, 0.18) * values
    return jnp.clip(values, min=-bound, max=bound).astype(held_as)


def setup_inputs(seed: int = 0, part: int = 0) -> dict:
    key_list = jax.random.split(jax.random.key(seed), 6)
    part_keys = jax.random.split(jax.random.fold_in(key_list[5], part), 6)
    return {
        "fields": centred(part_keys[0], (LEV, C, FACES, C), 1.0, 6.0, ((1, 64),), jnp.float32),
        "damp_four": jnp.clip(jnp.exp(jax.random.uniform(part_keys[1], (LEV,), jnp.float32, math.log(0.004), math.log(0.03))), 0.004, 0.03),
        "damp_six": jnp.clip(jnp.exp(jax.random.uniform(part_keys[2], (LEV,), jnp.float32, math.log(0.0008), math.log(0.006))), 0.0008, 0.006),
        "metric": jnp.clip(1.0 + 0.18 * jax.random.normal(key_list[3], (4, C, FACES, C), jnp.float32), 0.1, 1.9),
        "seam_table": draw_seam_table(jax.random.fold_in(key_list[5], 71), part),
    }


def edge_cells(source):
    return jnp.stack([source[:, 0], jnp.transpose(source[:, :, :, -1], (0, 2, 1)), source[:, -1], jnp.transpose(source[:, :, :, 0], (0, 2, 1))], axis=2)


def seam_halo(edges, seam_table):
    neighbor = edges[:, seam_table[:, :, 0], seam_table[:, :, 1], :]
    flipped = (seam_table[:, :, 2] == 1)[None, :, :, None]
    return jnp.where(flipped, neighbor[..., ::-1], neighbor)


def laplace(source, metric, seam_table):
    halo_cells = seam_halo(edge_cells(source), seam_table)
    west_cells = jnp.transpose(halo_cells[:, :, 3], (0, 2, 1))[..., None]
    east_cells = jnp.transpose(halo_cells[:, :, 1], (0, 2, 1))[..., None]
    padded_x = jnp.concatenate([west_cells, source, east_cells], axis=3)
    padded_y = jnp.concatenate([halo_cells[:, None, :, 0], source, halo_cells[:, None, :, 2]], axis=1)
    return (metric[0] * (padded_x[..., :-2] - source) + metric[1] * (padded_x[..., 2:] - source)
            + metric[2] * (padded_y[:, :-2] - source) + metric[3] * (padded_y[:, 2:] - source))


def reference(fields, damp_four, damp_six, metric, seam_table):
    second = laplace(fields, metric, seam_table)
    fourth = laplace(second, metric, seam_table)
    sixth = laplace(fourth, metric, seam_table)
    return fields - damp_four[:, None, None, None] * fourth + damp_six[:, None, None, None] * sixth
```

```python
import functools

import jax
import jax.numpy as jnp
from jax import lax
from jax.experimental import pallas as pl
from jax.experimental.pallas import tpu as pltpu
from jax.sharding import PartitionSpec as P

MESH = pl.DeviceIdType.MESH
LANES = 128
PAD = 8
SOUTH, EAST, NORTH, WEST = 0, 1, 2, 3


def exact_dot(values, onehot):
    high = values.astype(jnp.bfloat16)
    rest = values - high.astype(jnp.float32)
    middle = rest.astype(jnp.bfloat16)
    low = (rest - middle.astype(jnp.float32)).astype(jnp.bfloat16)
    total = jnp.dot(low, onehot, preferred_element_type=jnp.float32)
    total = total + jnp.dot(middle, onehot, preferred_element_type=jnp.float32)
    return total + jnp.dot(high, onehot, preferred_element_type=jnp.float32)


def exact_left_dot(onehot, values):
    high = values.astype(jnp.bfloat16)
    rest = values - high.astype(jnp.float32)
    middle = rest.astype(jnp.bfloat16)
    low = (rest - middle.astype(jnp.float32)).astype(jnp.bfloat16)
    total = jnp.dot(onehot, low, preferred_element_type=jnp.float32)
    total = total + jnp.dot(onehot, middle, preferred_element_type=jnp.float32)
    return total + jnp.dot(onehot, high, preferred_element_type=jnp.float32)


def rows_reversed(block):
    count = block.shape[0]
    return jnp.concatenate([block[count - 1 - j : count - j] for j in range(count)], axis=0)


def level_eye(shape, code_row, source_code):
    row_lane = lax.broadcasted_iota(jnp.int32, shape, 0)
    column = lax.broadcasted_iota(jnp.int32, shape, 1)
    hit = (lax.shift_right_logical(row_lane, 3) == lax.shift_right_logical(column, 3)) & (
        code_row == jnp.bitwise_and(row_lane, 7) * 4 + source_code
    )
    return jnp.where(hit, 1.0, 0.0).astype(jnp.bfloat16)


def kernel(
    n, fields_hbm, metric_hbm, codes, damp_four, damp_six, out,
    f0, f1, f2, met, row_halo, own, mirror, piece_send, piece_all, piece_out, piece_in,
    stack, turned, rest_turned, extract, part, cell_metric, fix, fix_turned, k_halo, k_far,
    load_sem, row_send, row_recv, mir_send, mir_recv, far_send, far_recv, fan_send, fan_recv,
):
    levels, rows, faces, width = f0.shape
    blocks = width // LANES
    me = lax.axis_index("ty")
    last = n - 1
    at_first, at_last = me == 0, me == last
    special = jnp.logical_or(at_first, at_last)
    side = jnp.where(at_last, 1, 0)
    rim_row = side * (rows - 1)
    above, below = lax.rem(me + 1, n), lax.rem(me + last, n)
    opposite = last - me

    load_fields = pltpu.make_async_copy(fields_hbm, f0, load_sem.at[0])
    load_metric = pltpu.make_async_copy(metric_hbm, met, load_sem.at[1])
    load_fields.start()
    load_metric.start()

    barrier = pltpu.get_barrier_semaphore()

    def greet(device):
        pl.semaphore_signal(barrier, inc=1, device_id={"ty": device}, device_id_type=MESH)

    def spread(i):
        step = (i + 1) // 2
        return lax.rem(me + n // 2 + step * (1 - 2 * lax.rem(i, 2)) + n, n)

    @pl.when(special)
    def _():
        def one(i, _):
            greet(spread(i))
            return 0

        lax.fori_loop(0, last, one, 0)

    @pl.when(jnp.logical_not(at_first))
    def _():
        greet(0)

    @pl.when(jnp.logical_not(at_last))
    def _():
        greet(last)

    greet(above)
    greet(below)
    greet(opposite)

    stack[...] = jnp.zeros_like(stack)
    extract[...] = jnp.zeros_like(extract)
    fix[...] = jnp.zeros_like(fix)
    code_of = [codes[e : e + 1, :] for e in range(4)]
    reversed_south = codes[4:5, :] == 1
    reversed_north = codes[5:6, :] == 1
    square = (LANES, LANES)
    none = jnp.zeros(square, jnp.bfloat16)
    for index, (edge, to_west, to_east) in enumerate(
        ((WEST, 0, 1), (EAST, 1, 0), (WEST, 1, 0), (EAST, 0, 1), (SOUTH, 1, 1), (NORTH, 1, 1))
    ):
        span = slice(index * LANES, (index + 1) * LANES)
        k_halo[span, :LANES] = level_eye(square, code_of[WEST], edge) if to_west else none
        k_halo[span, LANES:] = level_eye(square, code_of[EAST], edge) if to_east else none
    for index, edge in enumerate((WEST, EAST)):
        span = slice(index * LANES, (index + 1) * LANES)
        k_far[span, :LANES] = level_eye(square, code_of[SOUTH], edge)
        k_far[span, LANES:] = level_eye(square, code_of[NORTH], edge)

    lane = lax.broadcasted_iota(jnp.int32, (faces, LANES), 1)
    wide_lane = lax.broadcasted_iota(jnp.int32, (faces, width), 1)

    def columns_of(west_tile, east_tile):
        total = jnp.zeros((faces, LANES), jnp.float32)
        for y in range(rows):
            total = jnp.where(lane == y, west_tile(y)[:, 0:1], total)
            total = jnp.where(lane == 16 + y, east_tile(y)[:, LANES - 1 : LANES], total)
        return total

    def turned_columns():
        table = extract[...].reshape(levels * PAD, LANES).T
        return table[0:rows], table[16 : 16 + rows]

    def take_columns(source):
        def one(level, _):
            extract[level, 0:faces, :] = columns_of(
                lambda y: source[level, y, :, 0:LANES],
                lambda y: source[level, y, :, width - LANES : width],
            )
            return 0

        lax.fori_loop(0, levels, one, 0)
        return turned_columns()

    def row_copy(round_, way):
        return pltpu.make_async_remote_copy(
            src_ref=(f0, f1, f2)[round_].at[:, 0 if way else rows - 1],
            dst_ref=row_halo.at[round_, way],
            send_sem=row_send.at[round_, way],
            recv_sem=row_recv.at[round_, way],
            device_id={"ty": below if way else above},
            device_id_type=MESH,
        )

    def mirror_copy(round_):
        return pltpu.make_async_remote_copy(
            src_ref=own.at[round_],
            dst_ref=mirror.at[round_],
            send_sem=mir_send.at[round_],
            recv_sem=mir_recv.at[round_],
            device_id={"ty": opposite},
            device_id_type=MESH,
        )

    def far_copy(round_, end):
        return pltpu.make_async_remote_copy(
            src_ref=piece_send.at[round_, end],
            dst_ref=piece_all.at[round_, me],
            send_sem=far_send.at[round_, end],
            recv_sem=far_recv.at[round_],
            device_id={"ty": last if end else 0},
            device_id_type=MESH,
        )

    def fan_copy(round_, device):
        return pltpu.make_async_remote_copy(
            src_ref=piece_out.at[round_, device],
            dst_ref=piece_in.at[round_, side],
            send_sem=fan_send.at[round_],
            recv_sem=fan_recv.at[round_, side],
            device_id={"ty": device},
            device_id_type=MESH,
        )

    def all_but_one(buffer, sem):
        return pltpu.make_async_copy(buffer.at[pl.ds(0, last)], buffer.at[pl.ds(0, last)], sem)

    def make_far_pieces(round_):
        west, east = own[round_, 0], own[round_, 1]
        straight = jnp.concatenate([west, east], axis=1)
        both = jnp.concatenate([straight, rows_reversed(straight)], axis=0)
        chosen = exact_dot(both, k_far[...])
        for end, flag in ((0, reversed_south), (1, reversed_north)):
            span = slice(end * LANES, (end + 1) * LANES)
            piece_send[round_, end] = jnp.where(flag, chosen[rows:, span], chosen[:rows, span])

    def send_columns(round_):
        mirror_copy(round_).start()
        make_far_pieces(round_)

        @pl.when(jnp.logical_not(at_first))
        def _():
            far_copy(round_, 0).start()

        @pl.when(jnp.logical_not(at_last))
        def _():
            far_copy(round_, 1).start()

        @pl.when(special)
        def _():
            piece_all[round_, me] = jnp.where(at_last, piece_send[round_, 1], piece_send[round_, 0])

    def send_rows(round_):
        row_copy(round_, 0).start()
        row_copy(round_, 1).start()

    def turn_stack(target):
        for b in range(blocks):
            span = slice(b * LANES, (b + 1) * LANES)
            target[span, :] = stack[:, :, span].reshape(levels * PAD, LANES).T

    def pack_fan(round_, source):
        stack[:, 0:faces, :] = source[:, rim_row]
        turn_stack(turned)
        flag = codes[pl.ds(4 + side, 1), :] == 1
        for j in range(n):
            here = turned[rows * j : rows * (j + 1), :]
            there = turned[rows * (last - j) : rows * (n - j), :]
            piece_out[round_, j] = jnp.where(flag, there, here)

        def one(i, _):
            fan_copy(round_, spread(i)).start()
            return 0

        lax.fori_loop(0, last, one, 0)
        piece_in[round_, side] = piece_out[round_, me]

    def local_seams(round_):
        code = codes[pl.ds(2 * side, 1), :]
        same = level_eye(square, code, 2 * side)
        other = level_eye(square, code, 2 - 2 * side)
        up = lax.broadcasted_iota(jnp.int32, square, 0)
        across = lax.broadcasted_iota(jnp.int32, square, 1)
        flip = jnp.where(up + across == LANES - 1, 1.0, 0.0).astype(jnp.bfloat16)
        stack[:, 0:faces, :] = row_halo[round_, side]
        turn_stack(rest_turned)
        for b in range(blocks):
            span = slice(b * LANES, (b + 1) * LANES)
            back = slice((blocks - 1 - b) * LANES, (blocks - b) * LANES)
            flipped = exact_left_dot(flip, turned[back, :])
            rest_turned[span, :] = exact_dot(flipped, same) + exact_dot(rest_turned[span, :], other)

    def join_far(round_):
        flag = codes[pl.ds(4 + side, 1), :] == 1
        for j in range(n):
            span = slice(rows * j, rows * (j + 1))
            rest_turned[span, :] += jnp.where(flag, piece_all[round_, last - j], piece_all[round_, j])
        for b in range(blocks):
            span = slice(b * LANES, (b + 1) * LANES)
            stack[:, :, span] = rest_turned[span, :].T.reshape(levels, PAD, LANES)

    def apply_interior(source, target, final):
        def one(level, _):
            cells = [source[level, y] for y in range(rows)]
            for y in range(rows):
                here = cells[y]
                west = jnp.where(wide_lane == 0, 0.0, pltpu.roll(here, 1, 1))
                east = jnp.where(wide_lane == width - 1, 0.0, pltpu.roll(here, width - 1, 1))
                south = cells[y - 1] if y > 0 else jnp.zeros_like(here)
                north = cells[y + 1] if y < rows - 1 else jnp.zeros_like(here)
                value = (
                    met[0, y] * (west - here)
                    + met[1, y] * (east - here)
                    + met[2, y] * (south - here)
                    + met[3, y] * (north - here)
                )
                if final:
                    value = f0[level, y] - damp_four[level] * here + damp_six[level] * value
                target[level, y] = value
            return 0

        lax.fori_loop(0, levels, one, 0)

    def add_row(target, y, weight, halo, final):
        def one(level, _):
            value = met[weight, y] * halo(level)
            if final:
                value = damp_six[level] * value
            target[level, y] += value
            return 0

        lax.fori_loop(0, levels, one, 0)

    def add_columns(target, which, final):
        def one(level, _):
            table = fix_turned[level, 0:faces, :]
            if final:
                table = table * damp_six[level]
            for y in which:
                target[level, y, :, 0:LANES] += jnp.where(lane == 0, table[:, y : y + 1], 0.0)
                target[level, y, :, width - LANES : width] += jnp.where(
                    lane == LANES - 1, table[:, 16 + y : 17 + y], 0.0
                )
            return 0

        lax.fori_loop(0, levels, one, 0)

    load_fields.wait()
    west, east = take_columns(f0)
    own[0, 0] = west
    own[0, 1] = east
    load_metric.wait()
    weights = columns_of(
        lambda y: met[0, y, :, 0:LANES], lambda y: met[1, y, :, width - LANES : width]
    )
    for level in range(levels):
        extract[level, 0:faces, :] = weights
    west, east = turned_columns()
    cell_metric[0] = west
    cell_metric[1] = east

    pl.semaphore_wait(
        barrier,
        3 + jnp.where(at_first, last, 1) + jnp.where(at_last, last, 1),
    )

    send_columns(0)
    send_rows(0)

    @pl.when(special)
    def _():
        pack_fan(0, f0)

    for round_ in range(3):
        source = (f0, f1, f2)[round_]
        target = (f1, f2, out)[round_]
        final = round_ == 2
        apply_interior(source, target, final)

        row_copy(round_, 0).wait_recv()
        row_copy(round_, 1).wait_recv()

        @pl.when(jnp.logical_not(at_first))
        def _():
            add_row(target, 0, 2, lambda level: row_halo[round_, 0, level], final)

        @pl.when(jnp.logical_not(at_last))
        def _():
            add_row(target, rows - 1, 3, lambda level: row_halo[round_, 1, level], final)

        @pl.when(special)
        def _():
            local_seams(round_)
            all_but_one(piece_all.at[round_], far_recv.at[round_]).wait()
            join_far(round_)
            add_row(target, rim_row, 2 + side, lambda level: stack[level, 0:faces, :], final)

        if not final:
            west, east = take_columns(target)
            part[0] = west
            part[1] = east

        mirror_copy(round_).wait_recv()

        @pl.when(jnp.logical_not(at_first))
        def _():
            pltpu.make_async_copy(piece_in.at[round_, 0], piece_in.at[round_, 0], fan_recv.at[round_, 0]).wait()

        @pl.when(jnp.logical_not(at_last))
        def _():
            pltpu.make_async_copy(piece_in.at[round_, 1], piece_in.at[round_, 1], fan_recv.at[round_, 1]).wait()

        from_south, from_north = piece_in[round_, 0], piece_in[round_, 1]
        candidates = jnp.concatenate(
            [
                own[round_, 0],
                own[round_, 1],
                rows_reversed(mirror[round_, 0]),
                rows_reversed(mirror[round_, 1]),
                jnp.where(reversed_south, rows_reversed(from_south), from_south),
                jnp.where(reversed_north, rows_reversed(from_north), from_north),
            ],
            axis=1,
        )
        halo = exact_dot(candidates, k_halo[...])
        west = cell_metric[0] * halo[:, :LANES]
        east = cell_metric[1] * halo[:, LANES:]
        if not final:
            own[round_ + 1, 0] = part[0] + west
            own[round_ + 1, 1] = part[1] + east
            send_columns(round_ + 1)
        fix[0:rows, :] = west
        fix[16 : 16 + rows, :] = east
        fix_turned[...] = fix[...].T.reshape(levels, PAD, LANES)
        if final:
            add_columns(target, range(rows), True)
        else:
            add_columns(target, (0, rows - 1), False)
            send_rows(round_ + 1)

            @pl.when(special)
            def _():
                pack_fan(round_ + 1, target)

            add_columns(target, range(1, rows - 1), False)

    for round_ in range(3):
        row_copy(round_, 0).wait_send()
        row_copy(round_, 1).wait_send()
        mirror_copy(round_).wait_send()

        @pl.when(jnp.logical_not(at_first))
        def _():
            far_copy(round_, 0).wait_send()

        @pl.when(jnp.logical_not(at_last))
        def _():
            far_copy(round_, 1).wait_send()

        @pl.when(special)
        def _():
            all_but_one(piece_out.at[round_], fan_send.at[round_]).wait()


def code_rows(seam_table, levels):
    joined = seam_table[:, :, 0] * 4 + seam_table[:, :, 1]
    table = jnp.concatenate([joined.T, seam_table[:, 0:3:2, 2].T], axis=0)
    table = jnp.pad(table, ((0, 2), (0, PAD - table.shape[1])), constant_values=-1)
    return jnp.tile(table, (1, levels))


def solution(mesh):
    n = mesh.shape["ty"]

    def per_device(fields, damp_four, damp_six, metric, seam_table):
        levels, rows, faces, width = fields.shape
        f32, bf16 = jnp.float32, jnp.bfloat16
        vmem, dma = pltpu.VMEM, pltpu.SemaphoreType.DMA
        any_space = pl.BlockSpec(memory_space=pl.ANY)
        in_smem = pl.BlockSpec(memory_space=pltpu.SMEM)
        in_vmem = pl.BlockSpec(memory_space=pltpu.VMEM)
        return pl.pallas_call(
            functools.partial(kernel, n),
            out_shape=jax.ShapeDtypeStruct(fields.shape, f32),
            in_specs=[any_space, any_space, in_vmem, in_smem, in_smem],
            out_specs=in_vmem,
            scratch_shapes=[
                vmem(fields.shape, f32),
                vmem(fields.shape, f32),
                vmem(fields.shape, f32),
                vmem(metric.shape, f32),
                vmem((3, 2, levels, faces, width), f32),
                vmem((3, 2, rows, LANES), f32),
                vmem((3, 2, rows, LANES), f32),
                vmem((3, 2, rows, LANES), f32),
                vmem((3, n, rows, LANES), f32),
                vmem((3, n, rows, LANES), f32),
                vmem((3, 2, rows, LANES), f32),
                vmem((levels, PAD, width), f32),
                vmem((width, LANES), f32),
                vmem((width, LANES), f32),
                vmem((levels, PAD, LANES), f32),
                vmem((2, rows, LANES), f32),
                vmem((2, rows, LANES), f32),
                vmem((LANES, LANES), f32),
                vmem((levels, PAD, LANES), f32),
                vmem((6 * LANES, 2 * LANES), bf16),
                vmem((2 * LANES, 2 * LANES), bf16),
                dma((2,)),
                dma((3, 2)),
                dma((3, 2)),
                dma((3,)),
                dma((3,)),
                dma((3, 2)),
                dma((3,)),
                dma((3,)),
                dma((3, 2)),
            ],
            compiler_params=pltpu.CompilerParams(
                collective_id=0, has_side_effects=True, vmem_limit_bytes=60 * 1024 * 1024
            ),
        )(fields, metric, code_rows(seam_table, levels), damp_four, damp_six)

    placed = (
        P("member", "ty", None, None),
        P("member"),
        P("member"),
        P(None, "ty", None, None),
        P(),
    )
    return jax.shard_map(
        per_device,
        mesh=mesh,
        in_specs=placed,
        out_specs=P("member", "ty", None, None),
        check_vma=False,
    )
```

```python
import functools

import jax
import jax.numpy as jnp
from jax import lax
from jax.experimental import pallas as pl
from jax.experimental.pallas import tpu as pltpu
from jax.sharding import PartitionSpec as P

MESH = pl.DeviceIdType.MESH
LANES = 128
PAD = 8
SOUTH, EAST, NORTH, WEST = 0, 1, 2, 3


def three_parts(values):
    high = values.astype(jnp.bfloat16).astype(jnp.float32)
    rest = values - high
    middle = rest.astype(jnp.bfloat16).astype(jnp.float32)
    return high, middle, rest - middle


def exact_dot(values, onehot):
    count = values.shape[0]
    short = -count % 8
    if short:
        values = jnp.concatenate([values, jnp.zeros((short, values.shape[1]), jnp.float32)], axis=0)
    whole = count + short
    stacked = jnp.concatenate(three_parts(values), axis=0).astype(jnp.bfloat16)
    product = jnp.dot(stacked, onehot, preferred_element_type=jnp.float32)
    total = product[2 * whole :] + product[whole : 2 * whole] + product[:whole]
    return total[:count]


def exact_left_dot(onehot, values):
    wide = values.shape[1]
    stacked = jnp.concatenate(three_parts(values), axis=1).astype(jnp.bfloat16)
    product = jnp.dot(onehot, stacked, preferred_element_type=jnp.float32)
    return product[:, 2 * wide :] + product[:, wide : 2 * wide] + product[:, :wide]


def rows_reversed(block):
    count = block.shape[0]
    return jnp.concatenate([block[count - 1 - j : count - j] for j in range(count)], axis=0)


def level_eye(shape, code_row, source_code, shift):
    row_lane = lax.broadcasted_iota(jnp.int32, shape, 0)
    column = lax.broadcasted_iota(jnp.int32, shape, 1)
    level = (1 << shift) - 1
    hit = (jnp.bitwise_and(row_lane, level) == jnp.bitwise_and(column, level)) & (
        code_row == lax.shift_right_logical(row_lane, shift) * 4 + source_code
    )
    return jnp.where(hit, 1.0, 0.0).astype(jnp.bfloat16)


def kernel(
    n, fields_hbm, metric_hbm, seam, damp_four, damp_six, out_hbm,
    f0, f1, f2, out, met, row_halo, own, mirror, piece_send, piece_all, piece_out, piece_in,
    stack, turned, turned_part, rim_weight, rest, extract, part, cell_metric, corner_metric,
    fix, fix_turned, k_halo, k_far, codes, damp,
    load_sem, store_sem, row_send, row_recv, mir_send, mir_recv, far_send, far_recv, fan_send, fan_recv,
):
    rows, faces, levels, width = f0.shape
    shift = levels.bit_length() - 1
    blocks = width // LANES
    me = lax.axis_index("ty")
    last = n - 1
    at_first, at_last = me == 0, me == last
    special = jnp.logical_or(at_first, at_last)
    side = jnp.where(at_last, 1, 0)
    rim_row = side * (rows - 1)
    above, below = lax.rem(me + 1, n), lax.rem(me + last, n)
    opposite = last - me

    load_fields = pltpu.make_async_copy(fields_hbm, f0, load_sem.at[0])
    load_metric = pltpu.make_async_copy(metric_hbm, met, load_sem.at[1])
    load_fields.start()
    load_metric.start()

    barrier = pltpu.get_barrier_semaphore()

    def greet(device):
        pl.semaphore_signal(barrier, inc=1, device_id={"ty": device}, device_id_type=MESH)

    def spread(i):
        step = (i + 1) // 2
        return lax.rem(me + n // 2 + step * (1 - 2 * lax.rem(i, 2)) + n, n)

    @pl.when(special)
    def _():
        def one(i, _):
            greet(spread(i))
            return 0

        lax.fori_loop(0, last, one, 0)

    @pl.when(jnp.logical_not(at_first))
    def _():
        greet(0)

    @pl.when(jnp.logical_not(at_last))
    def _():
        greet(last)

    greet(above)
    greet(below)
    greet(opposite)

    stack[...] = jnp.zeros_like(stack)
    extract[...] = jnp.zeros_like(extract)
    fix[...] = jnp.zeros_like(fix)
    face_of_lane = lax.shift_right_logical(lax.broadcasted_iota(jnp.int32, (1, LANES), 1), shift)

    def lane_row(entry):
        total = jnp.full((1, LANES), -1, jnp.int32)
        for face in range(faces):
            total = jnp.where(face_of_lane == face, entry(face), total)
        return total

    code_of = [lane_row(lambda f, e=e: seam[0, e, f] * 4 + seam[1, e, f]) for e in range(4)]
    flags = [lane_row(lambda f, e=e: seam[2, e, f]) for e in (SOUTH, NORTH)]
    for index, row in enumerate((code_of[SOUTH], code_of[NORTH], flags[0], flags[1])):
        codes[index : index + 1, :] = row
    reversed_south, reversed_north = flags[0] == 1, flags[1] == 1
    square = (LANES, LANES)
    none = jnp.zeros(square, jnp.bfloat16)
    for index, (edge, to_west, to_east) in enumerate(
        ((WEST, 0, 1), (EAST, 1, 0), (WEST, 1, 0), (EAST, 0, 1), (SOUTH, 1, 1), (NORTH, 1, 1))
    ):
        span = slice(index * LANES, (index + 1) * LANES)
        k_halo[span, :LANES] = level_eye(square, code_of[WEST], edge, shift) if to_west else none
        k_halo[span, LANES:] = level_eye(square, code_of[EAST], edge, shift) if to_east else none
    for index, edge in enumerate((WEST, EAST)):
        span = slice(index * LANES, (index + 1) * LANES)
        k_far[span, :LANES] = level_eye(square, code_of[SOUTH], edge, shift)
        k_far[span, LANES:] = level_eye(square, code_of[NORTH], edge, shift)
    level_row = lax.broadcasted_iota(jnp.int32, (levels, LANES), 0)
    for index, source in enumerate((damp_four, damp_six)):
        total = jnp.zeros((levels, LANES), jnp.float32)
        for level in range(levels):
            total = jnp.where(level_row == level, source[level], total)
        damp[index] = total

    lane = lax.broadcasted_iota(jnp.int32, (levels, LANES), 1)
    wide_lane = lax.broadcasted_iota(jnp.int32, (8, width), 1)

    def columns_of(west_tile, east_tile):
        total = jnp.zeros((levels, LANES), jnp.float32)
        for y in range(rows):
            total = jnp.where(lane == y, west_tile(y), total)
            total = jnp.where(lane == 16 + y, east_tile(y), total)
        return total

    def turned_columns():
        return extract[...].reshape(LANES, LANES).T

    def take_columns(source):
        def one(face, _):
            extract[face] = columns_of(
                lambda y: source[y, face, :, 0:LANES][:, 0:1],
                lambda y: source[y, face, :, width - LANES : width][:, LANES - 1 : LANES],
            )
            return 0

        lax.fori_loop(0, faces, one, 0)
        table = turned_columns()
        return table[0:rows], table[16 : 16 + rows]

    def row_copy(round_, way):
        return pltpu.make_async_remote_copy(
            src_ref=(f0, f1, f2)[round_].at[0 if way else rows - 1],
            dst_ref=row_halo.at[round_, way],
            send_sem=row_send.at[round_, way],
            recv_sem=row_recv.at[round_, way],
            device_id={"ty": below if way else above},
            device_id_type=MESH,
        )

    def mirror_copy(round_):
        return pltpu.make_async_remote_copy(
            src_ref=own.at[round_],
            dst_ref=mirror.at[round_],
            send_sem=mir_send.at[round_],
            recv_sem=mir_recv.at[round_],
            device_id={"ty": opposite},
            device_id_type=MESH,
        )

    def far_copy(round_, end):
        return pltpu.make_async_remote_copy(
            src_ref=piece_send.at[round_, end],
            dst_ref=piece_all.at[round_, me],
            send_sem=far_send.at[round_, end],
            recv_sem=far_recv.at[round_],
            device_id={"ty": last if end else 0},
            device_id_type=MESH,
        )

    def fan_copy(round_, device):
        return pltpu.make_async_remote_copy(
            src_ref=piece_out.at[round_, device],
            dst_ref=piece_in.at[round_, side],
            send_sem=fan_send.at[round_],
            recv_sem=fan_recv.at[round_, side],
            device_id={"ty": device},
            device_id_type=MESH,
        )

    def all_but_one(buffer, sem):
        return pltpu.make_async_copy(buffer.at[pl.ds(0, last)], buffer.at[pl.ds(0, last)], sem)

    def make_far_pieces(round_):
        straight = jnp.concatenate([own[round_, 0], own[round_, 1]], axis=1)
        both = jnp.concatenate([straight, rows_reversed(straight)], axis=0)
        chosen = exact_dot(both, k_far[...])
        for end, flag in ((0, reversed_south), (1, reversed_north)):
            span = slice(end * LANES, (end + 1) * LANES)
            piece_send[round_, end] = jnp.where(flag, chosen[rows:, span], chosen[:rows, span])

    def send_columns(round_):
        @pl.when(jnp.logical_not(at_first))
        def _():
            far_copy(round_, 0).start()

        @pl.when(jnp.logical_not(at_last))
        def _():
            far_copy(round_, 1).start()

        mirror_copy(round_).start()

        @pl.when(special)
        def _():
            piece_all[round_, me] = jnp.where(at_last, piece_send[round_, 1], piece_send[round_, 0])

    def send_rows(round_):
        row_copy(round_, 0).start()
        row_copy(round_, 1).start()

    def turn_into(target, planes):
        stack[0:faces] = planes
        for b in range(blocks):
            span = slice(b * LANES, (b + 1) * LANES)
            target[span, :] = stack[:, :, span].reshape(LANES, LANES).T

    def pack_fan(round_):
        flag = codes[pl.ds(2 + side, 1), :] == 1
        for j in range(n):
            here = turned[rows * j : rows * (j + 1), :]
            there = turned[rows * (last - j) : rows * (n - j), :]
            piece_out[round_, j] = jnp.where(flag, there, here)

    def send_fan(round_):
        def one(i, _):
            fan_copy(round_, spread(i)).start()
            return 0

        lax.fori_loop(0, last, one, 0)
        piece_in[round_, side] = piece_out[round_, me]

    def local_seams(round_):
        code = codes[pl.ds(side, 1), :]
        same = level_eye(square, code, 2 * side, shift)
        other = level_eye(square, code, 2 - 2 * side, shift)
        up = lax.broadcasted_iota(jnp.int32, square, 0)
        across = lax.broadcasted_iota(jnp.int32, square, 1)
        flip = jnp.where(up + across == LANES - 1, 1.0, 0.0).astype(jnp.bfloat16)
        turn_into(rest, row_halo[round_, side])
        for b in range(blocks):
            span = slice(b * LANES, (b + 1) * LANES)
            back = slice((blocks - 1 - b) * LANES, (blocks - b) * LANES)
            flipped = exact_left_dot(flip, turned[back, :])
            rest[span, :] = exact_dot(flipped, same) + exact_dot(rest[span, :], other)

    def join_far(round_):
        flag = codes[pl.ds(2 + side, 1), :] == 1
        for j in range(n):
            span = slice(rows * j, rows * (j + 1))
            rest[span, :] += jnp.where(flag, piece_all[round_, last - j], piece_all[round_, j])

    def apply_interior(source, target, final):
        halves = levels // 8

        def one(step, _):
            face = step // halves
            some = pl.ds(pl.multiple_of(lax.rem(step, halves) * 8, 8), 8)
            cells = [source[y, face, some, :] for y in range(rows)]
            if final:
                four = jnp.concatenate([damp[0, some, :]] * blocks, axis=1)
                six = jnp.concatenate([damp[1, some, :]] * blocks, axis=1)
            for y in range(rows):
                here = cells[y]
                west = jnp.where(wide_lane == 0, 0.0, pltpu.roll(here, 1, 1))
                east = jnp.where(wide_lane == width - 1, 0.0, pltpu.roll(here, width - 1, 1))
                south = cells[y - 1] if y > 0 else jnp.zeros_like(here)
                north = cells[y + 1] if y < rows - 1 else jnp.zeros_like(here)
                value = (
                    met[y, face, 0:1, :] * (west - here)
                    + met[y, face, 1:2, :] * (east - here)
                    + met[y, face, 2:3, :] * (south - here)
                    + met[y, face, 3:4, :] * (north - here)
                )
                if final:
                    value = f0[y, face, some, :] - four * here + six * value
                target[y, face, some, :] = value
            return 0

        lax.fori_loop(0, faces * halves, one, 0)

    def add_row(target, y, weight, halo, final):
        def one(face, _):
            value = met[y, face, pl.ds(weight, 1), :] * halo(face)
            if final:
                value = jnp.concatenate([damp[1]] * blocks, axis=1) * value
            target[y, face] += value
            return 0

        lax.fori_loop(0, faces, one, 0)

    def add_columns(target, which, final):
        def one(face, _):
            table = fix_turned[face]
            if final:
                table = table * damp[1]
            for y in which:
                target[y, face, :, 0:LANES] += jnp.where(lane == 0, table[:, y : y + 1], 0.0)
                target[y, face, :, width - LANES : width] += jnp.where(
                    lane == LANES - 1, table[:, 16 + y : 17 + y], 0.0
                )
            return 0

        lax.fori_loop(0, faces, one, 0)

    middle = pl.ds(LANES, width - 2 * LANES)

    def store_copy(index):
        if index == 0:
            span = (pl.ds(1, rows - 2), slice(None), slice(None), middle)
        elif index < 3:
            span = ((0, rows - 1)[index - 1], slice(None), slice(None), middle)
        else:
            span = (slice(None), slice(None), slice(None), pl.ds((0, width - LANES)[index - 3], LANES))
        return pltpu.make_async_copy(out.at[span], out_hbm.at[span], store_sem.at[index])

    load_fields.wait()
    west, east = take_columns(f0)
    own[0, 0] = west
    own[0, 1] = east
    make_far_pieces(0)
    load_metric.wait()
    for face in range(faces):
        weights = columns_of(
            lambda y: met[y, face, 0:1, 0:LANES][:, 0:1],
            lambda y: met[y, face, 1:2, width - LANES : width][:, LANES - 1 : LANES],
        )
        rim = met[rim_row, face, pl.ds(2 + side, 1), :]
        weights = jnp.where(lane == 32, rim[:, 0:1], weights)
        extract[face] = jnp.where(lane == 33, rim[:, width - 1 : width], weights)
    table = turned_columns()
    cell_metric[0] = table[0:rows]
    cell_metric[1] = table[16 : 16 + rows]
    corner_metric[0] = table[32:33]
    corner_metric[1] = table[33:34]

    @pl.when(special)
    def _():
        for face in range(faces):
            stack[face] = jnp.broadcast_to(met[rim_row, face, pl.ds(2 + side, 1), :], (levels, width))
        for b in range(blocks):
            span = slice(b * LANES, (b + 1) * LANES)
            rim_weight[span, :] = stack[:, :, span].reshape(LANES, LANES).T
        turn_into(turned, f0[rim_row])
        pack_fan(0)

    pl.semaphore_wait(
        barrier,
        3 + jnp.where(at_first, last, 1) + jnp.where(at_last, last, 1),
    )

    send_columns(0)

    @pl.when(special)
    def _():
        send_fan(0)

    send_rows(0)

    for round_ in range(3):
        source = (f0, f1, f2)[round_]
        target = (f1, f2, out)[round_]
        final = round_ == 2
        apply_interior(source, target, final)
        if final:
            store_copy(0).start()

        row_copy(round_, 0).wait_recv()
        row_copy(round_, 1).wait_recv()

        @pl.when(jnp.logical_not(at_first))
        def _():
            add_row(target, 0, 2, lambda face: row_halo[round_, 0, face], final)

        @pl.when(jnp.logical_not(at_last))
        def _():
            add_row(target, rows - 1, 3, lambda face: row_halo[round_, 1, face], final)

        if not final:
            west, east = take_columns(target)
            part[0] = west
            part[1] = east

        @pl.when(special)
        def _():
            local_seams(round_)
            if not final:
                turn_into(turned_part, target[rim_row])
            all_but_one(piece_all.at[round_], far_recv.at[round_]).wait()
            join_far(round_)
            if not final:
                part[0, pl.ds(rim_row, 1), :] += corner_metric[0] * rest[0:1, :]
                part[1, pl.ds(rim_row, 1), :] += corner_metric[1] * rest[width - 1 : width, :]

        mirror_copy(round_).wait_recv()

        @pl.when(jnp.logical_not(at_first))
        def _():
            pltpu.make_async_copy(piece_in.at[round_, 0], piece_in.at[round_, 0], fan_recv.at[round_, 0]).wait()

        @pl.when(jnp.logical_not(at_last))
        def _():
            pltpu.make_async_copy(piece_in.at[round_, 1], piece_in.at[round_, 1], fan_recv.at[round_, 1]).wait()

        from_south, from_north = piece_in[round_, 0], piece_in[round_, 1]
        candidates = jnp.concatenate(
            [
                own[round_, 0],
                own[round_, 1],
                rows_reversed(mirror[round_, 0]),
                rows_reversed(mirror[round_, 1]),
                jnp.where(reversed_south, rows_reversed(from_south), from_south),
                jnp.where(reversed_north, rows_reversed(from_north), from_north),
            ],
            axis=1,
        )
        halo = exact_dot(candidates, k_halo[...])
        west = cell_metric[0] * halo[:, :LANES]
        east = cell_metric[1] * halo[:, LANES:]
        fix[0:rows, :] = west
        fix[16 : 16 + rows, :] = east
        if not final:
            own[round_ + 1, 0] = part[0] + west
            own[round_ + 1, 1] = part[1] + east
            make_far_pieces(round_ + 1)
            send_columns(round_ + 1)

            @pl.when(special)
            def _():
                turned[...] = turned_part[...] + rim_weight[...] * rest[...]
                turned[0:1, :] += fix[pl.ds(rim_row, 1), :]
                turned[width - 1 : width, :] += fix[pl.ds(16 + rim_row, 1), :]
                pack_fan(round_ + 1)
                send_fan(round_ + 1)

        @pl.when(special)
        def _():
            for b in range(blocks):
                span = slice(b * LANES, (b + 1) * LANES)
                stack[:, :, span] = rest[span, :].T.reshape(PAD, levels, LANES)
            add_row(target, rim_row, 2 + side, lambda face: stack[face], final)

        fix_turned[...] = fix[...].T.reshape(PAD, levels, LANES)
        if final:
            store_copy(1).start()
            store_copy(2).start()
            add_columns(target, range(rows), True)
            store_copy(3).start()
            store_copy(4).start()
        else:
            add_columns(target, (0, rows - 1), False)
            send_rows(round_ + 1)
            add_columns(target, range(1, rows - 1), False)

    for round_ in range(3):
        row_copy(round_, 0).wait_send()
        row_copy(round_, 1).wait_send()
        mirror_copy(round_).wait_send()

        @pl.when(jnp.logical_not(at_first))
        def _():
            far_copy(round_, 0).wait_send()

        @pl.when(jnp.logical_not(at_last))
        def _():
            far_copy(round_, 1).wait_send()

        @pl.when(special)
        def _():
            all_but_one(piece_out.at[round_], fan_send.at[round_]).wait()

    for index in range(5):
        store_copy(index).wait()


def solution(mesh):
    n = mesh.shape["ty"]

    def per_device(fields, damp_four, damp_six, metric, seam_table):
        fields = jnp.transpose(fields, (1, 2, 0, 3))
        metric = jnp.transpose(metric, (1, 2, 0, 3))
        rows, faces, levels, width = fields.shape
        f32, bf16 = jnp.float32, jnp.bfloat16
        vmem, dma = pltpu.VMEM, pltpu.SemaphoreType.DMA
        any_space = pl.BlockSpec(memory_space=pl.ANY)
        in_smem = pl.BlockSpec(memory_space=pltpu.SMEM)
        result = pl.pallas_call(
            functools.partial(kernel, n),
            out_shape=jax.ShapeDtypeStruct(fields.shape, f32),
            in_specs=[any_space, any_space, in_smem, in_smem, in_smem],
            out_specs=any_space,
            scratch_shapes=[
                vmem(fields.shape, f32),
                vmem(fields.shape, f32),
                vmem(fields.shape, f32),
                vmem(fields.shape, f32),
                vmem(metric.shape, f32),
                vmem((3, 2, faces, levels, width), f32),
                vmem((3, 2, rows, LANES), f32),
                vmem((3, 2, rows, LANES), f32),
                vmem((3, 2, rows, LANES), f32),
                vmem((3, n, rows, LANES), f32),
                vmem((3, n, rows, LANES), f32),
                vmem((3, 2, rows, LANES), f32),
                vmem((PAD, levels, width), f32),
                vmem((width, LANES), f32),
                vmem((width, LANES), f32),
                vmem((width, LANES), f32),
                vmem((width, LANES), f32),
                vmem((PAD, levels, LANES), f32),
                vmem((2, rows, LANES), f32),
                vmem((2, rows, LANES), f32),
                vmem((2, 1, LANES), f32),
                vmem((LANES, LANES), f32),
                vmem((PAD, levels, LANES), f32),
                vmem((6 * LANES, 2 * LANES), bf16),
                vmem((2 * LANES, 2 * LANES), bf16),
                vmem((8, LANES), jnp.int32),
                vmem((2, levels, LANES), f32),
                dma((2,)),
                dma((5,)),
                dma((3, 2)),
                dma((3, 2)),
                dma((3,)),
                dma((3,)),
                dma((3, 2)),
                dma((3,)),
                dma((3,)),
                dma((3, 2)),
            ],
            compiler_params=pltpu.CompilerParams(
                collective_id=0, has_side_effects=True, vmem_limit_bytes=60 * 1024 * 1024
            ),
        )(fields, metric, jnp.transpose(seam_table, (2, 1, 0)), damp_four, damp_six)
        return jnp.transpose(result, (2, 0, 1, 3))

    placed = (
        P("member", "ty", None, None),
        P("member"),
        P("member"),
        P(None, "ty", None, None),
        P(),
    )
    return jax.shard_map(
        per_device,
        mesh=mesh,
        in_specs=placed,
        out_specs=P("member", "ty", None, None),
        check_vma=False,
    )
```

```python
import functools

import jax
import jax.numpy as jnp
from jax import lax
from jax.experimental import pallas as pl
from jax.experimental.pallas import tpu as pltpu
from jax.sharding import PartitionSpec as P

MESH = pl.DeviceIdType.MESH
LANES = 128
PAD = 8
SOUTH, EAST, NORTH, WEST = 0, 1, 2, 3


def three_parts(values):
    high = values.astype(jnp.bfloat16).astype(jnp.float32)
    rest = values - high
    middle = rest.astype(jnp.bfloat16).astype(jnp.float32)
    return high, middle, rest - middle


def exact_dot(values, onehot):
    count = values.shape[0]
    short = -count % 8
    if short:
        values = jnp.concatenate([values, jnp.zeros((short, values.shape[1]), jnp.float32)], axis=0)
    whole = count + short
    stacked = jnp.concatenate(three_parts(values), axis=0).astype(jnp.bfloat16)
    product = jnp.dot(stacked, onehot, preferred_element_type=jnp.float32)
    total = product[2 * whole :] + product[whole : 2 * whole] + product[:whole]
    return total[:count]


def exact_left_dot(onehot, values):
    wide = values.shape[1]
    stacked = jnp.concatenate(three_parts(values), axis=1).astype(jnp.bfloat16)
    product = jnp.dot(onehot, stacked, preferred_element_type=jnp.float32)
    return product[:, 2 * wide :] + product[:, wide : 2 * wide] + product[:, :wide]


def rows_reversed(block):
    count = block.shape[0]
    return jnp.concatenate([block[count - 1 - j : count - j] for j in range(count)], axis=0)


def level_eye(shape, code_row, source_code, shift):
    row_lane = lax.broadcasted_iota(jnp.int32, shape, 0)
    column = lax.broadcasted_iota(jnp.int32, shape, 1)
    level = (1 << shift) - 1
    hit = (jnp.bitwise_and(row_lane, level) == jnp.bitwise_and(column, level)) & (
        code_row == lax.shift_right_logical(row_lane, shift) * 4 + source_code
    )
    return jnp.where(hit, 1.0, 0.0).astype(jnp.bfloat16)


def kernel(
    n, fields_hbm, metric_hbm, seam, damp_four, damp_six, out_hbm,
    f0, f1, f2, out, met, row_halo, own, mirror, piece_send, piece_all, piece_out, piece_in,
    stack, turned, rest, picks, part_pieces, weight_pieces, relayed, extract, part, cell_metric, corner_metric,
    fix, fix_turned, k_halo, k_far, codes, damp,
    load_sem, store_sem, row_send, row_recv, mir_send, mir_recv, far_send, far_recv, fan_send, fan_recv,
    relay_send, relay_recv,
):
    rows, faces, levels, width = f0.shape
    shift = levels.bit_length() - 1
    blocks = width // LANES
    me = lax.axis_index("ty")
    last = n - 1
    at_first, at_last = me == 0, me == last
    special = jnp.logical_or(at_first, at_last)
    side = jnp.where(at_last, 1, 0)
    rim_row = side * (rows - 1)
    above, below = lax.rem(me + 1, n), lax.rem(me + last, n)
    opposite = last - me

    reach, stride = 3 * n // 16, n // 4

    def in_lower(device):
        return jnp.logical_and(device >= n // 2 - reach, device < n // 2)

    def in_upper(device):
        return jnp.logical_and(device >= n // 2, device < n // 2 + reach)

    middle_strip = jnp.logical_or(in_lower(me), in_upper(me))
    helper = jnp.where(in_lower(me), me - stride, me + stride)
    helps = jnp.logical_or(in_lower(me + stride), in_upper(me - stride))
    client = jnp.where(in_lower(me + stride), me + stride, me - stride)

    load_fields = pltpu.make_async_copy(fields_hbm, f0, load_sem.at[0])
    load_metric = pltpu.make_async_copy(metric_hbm, met, load_sem.at[1])
    load_fields.start()
    load_metric.start()

    barrier = pltpu.get_barrier_semaphore()

    def greet(device):
        pl.semaphore_signal(barrier, inc=1, device_id={"ty": device}, device_id_type=MESH)

    def spread(i):
        step = (i + 1) // 2
        return lax.rem(me + n // 2 + step * (1 - 2 * lax.rem(i, 2)) + n, n)

    @pl.when(special)
    def _():
        def one(i, _):
            device = spread(i)
            skipped = jnp.logical_or(in_lower(device), in_upper(device))

            @pl.when(jnp.logical_or(at_first, jnp.logical_not(skipped)))
            def _():
                greet(device)

            return 0

        lax.fori_loop(0, last, one, 0)

    @pl.when(jnp.logical_not(at_first))
    def _():
        greet(0)

    @pl.when(jnp.logical_not(at_last))
    def _():
        greet(last)

    @pl.when(helps)
    def _():
        greet(client)

    greet(above)
    greet(below)
    greet(opposite)

    stack[...] = jnp.zeros_like(stack)
    extract[...] = jnp.zeros_like(extract)
    fix[...] = jnp.zeros_like(fix)
    face_of_lane = lax.shift_right_logical(lax.broadcasted_iota(jnp.int32, (1, LANES), 1), shift)

    def lane_row(entry):
        total = jnp.full((1, LANES), -1, jnp.int32)
        for face in range(faces):
            total = jnp.where(face_of_lane == face, entry(face), total)
        return total

    code_of = [lane_row(lambda f, e=e: seam[0, e, f] * 4 + seam[1, e, f]) for e in range(4)]
    flags = [lane_row(lambda f, e=e: seam[2, e, f]) for e in (SOUTH, NORTH)]
    for index, row in enumerate((code_of[SOUTH], code_of[NORTH], flags[0], flags[1])):
        codes[index : index + 1, :] = row
    reversed_south, reversed_north = flags[0] == 1, flags[1] == 1
    square = (LANES, LANES)
    none = jnp.zeros(square, jnp.bfloat16)
    for index, (edge, to_west, to_east) in enumerate(
        ((WEST, 0, 1), (EAST, 1, 0), (WEST, 1, 0), (EAST, 0, 1), (SOUTH, 1, 1), (NORTH, 1, 1))
    ):
        span = slice(index * LANES, (index + 1) * LANES)
        k_halo[span, :LANES] = level_eye(square, code_of[WEST], edge, shift) if to_west else none
        k_halo[span, LANES:] = level_eye(square, code_of[EAST], edge, shift) if to_east else none
    for index, edge in enumerate((WEST, EAST)):
        span = slice(index * LANES, (index + 1) * LANES)
        k_far[span, :LANES] = level_eye(square, code_of[SOUTH], edge, shift)
        k_far[span, LANES:] = level_eye(square, code_of[NORTH], edge, shift)
    level_row = lax.broadcasted_iota(jnp.int32, (levels, LANES), 0)
    for index, source in enumerate((damp_four, damp_six)):
        total = jnp.zeros((levels, LANES), jnp.float32)
        for level in range(levels):
            total = jnp.where(level_row == level, source[level], total)
        damp[index] = total

    lane = lax.broadcasted_iota(jnp.int32, (levels, LANES), 1)
    wide_lane = lax.broadcasted_iota(jnp.int32, (8, width), 1)

    def columns_of(west_tile, east_tile):
        total = jnp.zeros((levels, LANES), jnp.float32)
        for y in range(rows):
            total = jnp.where(lane == y, west_tile(y), total)
            total = jnp.where(lane == 16 + y, east_tile(y), total)
        return total

    def turned_columns():
        return extract[...].reshape(LANES, LANES).T

    def take_columns(source):
        def one(face, _):
            extract[face] = columns_of(
                lambda y: source[y, face, :, 0:LANES][:, 0:1],
                lambda y: source[y, face, :, width - LANES : width][:, LANES - 1 : LANES],
            )
            return 0

        lax.fori_loop(0, faces, one, 0)
        table = turned_columns()
        return table[0:rows], table[16 : 16 + rows]

    def row_copy(round_, way):
        return pltpu.make_async_remote_copy(
            src_ref=(f0, f1, f2)[round_].at[0 if way else rows - 1],
            dst_ref=row_halo.at[round_, way],
            send_sem=row_send.at[round_, way],
            recv_sem=row_recv.at[round_, way],
            device_id={"ty": below if way else above},
            device_id_type=MESH,
        )

    def mirror_copy(round_):
        return pltpu.make_async_remote_copy(
            src_ref=own.at[round_],
            dst_ref=mirror.at[round_],
            send_sem=mir_send.at[round_],
            recv_sem=mir_recv.at[round_],
            device_id={"ty": opposite},
            device_id_type=MESH,
        )

    def far_copy(round_, end):
        return pltpu.make_async_remote_copy(
            src_ref=piece_send.at[round_, end],
            dst_ref=piece_all.at[round_, me],
            send_sem=far_send.at[round_, end],
            recv_sem=far_recv.at[round_],
            device_id={"ty": last if end else 0},
            device_id_type=MESH,
        )

    def to_helper():
        return pltpu.make_async_remote_copy(
            src_ref=piece_send.at[0, 1],
            dst_ref=relayed,
            send_sem=far_send.at[0, 1],
            recv_sem=relay_recv,
            device_id={"ty": helper},
            device_id_type=MESH,
        )

    def for_client():
        return pltpu.make_async_remote_copy(
            src_ref=relayed,
            dst_ref=piece_all.at[0, client],
            send_sem=relay_send,
            recv_sem=far_recv.at[0],
            device_id={"ty": last},
            device_id_type=MESH,
        )

    def fan_copy(round_, device):
        return pltpu.make_async_remote_copy(
            src_ref=piece_out.at[round_, device],
            dst_ref=piece_in.at[round_, side],
            send_sem=fan_send.at[round_],
            recv_sem=fan_recv.at[round_, side],
            device_id={"ty": device},
            device_id_type=MESH,
        )

    def all_but_one(buffer, sem):
        return pltpu.make_async_copy(buffer.at[pl.ds(0, last)], buffer.at[pl.ds(0, last)], sem)

    def make_far_pieces(round_):
        straight = jnp.concatenate([own[round_, 0], own[round_, 1]], axis=1)
        both = jnp.concatenate([straight, rows_reversed(straight)], axis=0)
        chosen = exact_dot(both, k_far[...])
        for end, flag in ((0, reversed_south), (1, reversed_north)):
            span = slice(end * LANES, (end + 1) * LANES)
            piece_send[round_, end] = jnp.where(flag, chosen[rows:, span], chosen[:rows, span])

    def send_columns(round_):
        @pl.when(jnp.logical_not(at_first))
        def _():
            far_copy(round_, 0).start()

        if round_ == 0:
            @pl.when(middle_strip)
            def _():
                to_helper().start()

            @pl.when(jnp.logical_not(jnp.logical_or(middle_strip, at_last)))
            def _():
                far_copy(round_, 1).start()
        else:
            @pl.when(jnp.logical_not(at_last))
            def _():
                far_copy(round_, 1).start()

        mirror_copy(round_).start()

        @pl.when(special)
        def _():
            piece_all[round_, me] = jnp.where(at_last, piece_send[round_, 1], piece_send[round_, 0])

    def send_rows(round_):
        row_copy(round_, 0).start()
        row_copy(round_, 1).start()

    def turn_into(target, planes):
        stack[0:faces] = planes
        for b in range(blocks):
            span = slice(b * LANES, (b + 1) * LANES)
            target[span, :] = stack[:, :, span].reshape(LANES, LANES).T

    def pack_fan(round_):
        flag = codes[pl.ds(2 + side, 1), :] == 1
        for j in range(n):
            here = turned[rows * j : rows * (j + 1), :]
            there = turned[rows * (last - j) : rows * (n - j), :]
            piece_out[round_, j] = jnp.where(flag, there, here)

    def send_fan(round_):
        batch = max(k for k in range(1, 10) if (n - 1) % k == 0)

        def one(i, _):
            for k in range(batch):
                fan_copy(round_, spread(i * batch + k)).start()
            return 0

        lax.fori_loop(0, last // batch, one, 0)
        piece_in[round_, side] = piece_out[round_, me]

    def local_seams(round_, source, target, final):
        up = lax.broadcasted_iota(jnp.int32, square, 0)
        across = lax.broadcasted_iota(jnp.int32, square, 1)
        flip = jnp.where(up + across == LANES - 1, 1.0, 0.0).astype(jnp.bfloat16)
        picks[0] = source[rim_row]
        picks[1] = row_halo[round_, side]
        for face in range(faces):
            joined, edge = seam[0, 2 * side, face], seam[1, 2 * side, face]
            stack[face] = jnp.where(edge == 2 * side, picks[0, joined], 0.0)

        def flipped(b):
            span = slice(b * LANES, (b + 1) * LANES)
            return exact_dot(stack[:, :, span].reshape(LANES, LANES), flip).reshape(PAD, levels, LANES)

        for b in range((blocks + 1) // 2):
            c = blocks - 1 - b
            one, two = flipped(b), flipped(c)
            stack[:, :, c * LANES : (c + 1) * LANES] = one
            stack[:, :, b * LANES : (b + 1) * LANES] = two
        for face in range(faces):
            joined, edge = seam[0, 2 * side, face], seam[1, 2 * side, face]
            value = stack[face] + jnp.where(edge == 2 - 2 * side, picks[1, joined], 0.0)
            value = met[rim_row, face, pl.ds(2 + side, 1), :] * value
            if final:
                value = jnp.concatenate([damp[1]] * blocks, axis=1) * value
            target[rim_row, face] += value

    def join_far(round_):
        flag = codes[pl.ds(2 + side, 1), :] == 1
        for j in range(n):
            span = slice(rows * j, rows * (j + 1))
            rest[span, :] = jnp.where(flag, piece_all[round_, last - j], piece_all[round_, j])

    def pack_joined(round_):
        flag = codes[pl.ds(2 + side, 1), :] == 1
        row = lax.broadcasted_iota(jnp.int32, (rows, LANES), 0)
        for j in range(n // 2):
            k = last - j
            low, high = piece_all[round_, j], piece_all[round_, k]
            one = part_pieces[j] + weight_pieces[j] * jnp.where(flag, high, low)
            two = part_pieces[k] + weight_pieces[k] * jnp.where(flag, low, high)
            if j == 0:
                one = one + jnp.where(row == 0, fix[pl.ds(rim_row, 1), :], 0.0)
                two = two + jnp.where(row == rows - 1, fix[pl.ds(16 + rim_row, 1), :], 0.0)
            piece_out[round_ + 1, j] = jnp.where(flag, two, one)
            piece_out[round_ + 1, k] = jnp.where(flag, one, two)

    def cut(target, source):
        for j in range(n):
            target[j] = source[rows * j : rows * (j + 1), :]

    def apply_interior(source, target, final):
        halves = levels // 8

        def one(step, _):
            face = step // halves
            some = pl.ds(pl.multiple_of(lax.rem(step, halves) * 8, 8), 8)
            cells = [source[y, face, some, :] for y in range(rows)]
            if final:
                four = jnp.concatenate([damp[0, some, :]] * blocks, axis=1)
                six = jnp.concatenate([damp[1, some, :]] * blocks, axis=1)
            for y in range(rows):
                here = cells[y]
                west = jnp.where(wide_lane == 0, 0.0, pltpu.roll(here, 1, 1))
                east = jnp.where(wide_lane == width - 1, 0.0, pltpu.roll(here, width - 1, 1))
                south = cells[y - 1] if y > 0 else jnp.zeros_like(here)
                north = cells[y + 1] if y < rows - 1 else jnp.zeros_like(here)
                value = (
                    met[y, face, 0:1, :] * (west - here)
                    + met[y, face, 1:2, :] * (east - here)
                    + met[y, face, 2:3, :] * (south - here)
                    + met[y, face, 3:4, :] * (north - here)
                )
                if final:
                    value = f0[y, face, some, :] - four * here + six * value
                target[y, face, some, :] = value
            return 0

        lax.fori_loop(0, faces * halves, one, 0)

    def add_row(target, y, weight, halo, final):
        def one(face, _):
            value = met[y, face, pl.ds(weight, 1), :] * halo(face)
            if final:
                value = jnp.concatenate([damp[1]] * blocks, axis=1) * value
            target[y, face] += value
            return 0

        lax.fori_loop(0, faces, one, 0)

    def add_columns(target, which, final):
        def one(face, _):
            table = fix_turned[face]
            if final:
                table = table * damp[1]
            for y in which:
                target[y, face, :, 0:LANES] += jnp.where(lane == 0, table[:, y : y + 1], 0.0)
                target[y, face, :, width - LANES : width] += jnp.where(
                    lane == LANES - 1, table[:, 16 + y : 17 + y], 0.0
                )
            return 0

        lax.fori_loop(0, faces, one, 0)

    middle = pl.ds(LANES, width - 2 * LANES)

    def store_copy(index):
        if index == 0:
            span = (pl.ds(1, rows - 2), slice(None), slice(None), middle)
        elif index < 3:
            span = ((0, rows - 1)[index - 1], slice(None), slice(None), middle)
        else:
            span = (slice(None), slice(None), slice(None), pl.ds((0, width - LANES)[index - 3], LANES))
        return pltpu.make_async_copy(out.at[span], out_hbm.at[span], store_sem.at[index])

    load_fields.wait()
    west, east = take_columns(f0)
    own[0, 0] = west
    own[0, 1] = east
    make_far_pieces(0)
    load_metric.wait()
    for face in range(faces):
        weights = columns_of(
            lambda y: met[y, face, 0:1, 0:LANES][:, 0:1],
            lambda y: met[y, face, 1:2, width - LANES : width][:, LANES - 1 : LANES],
        )
        rim = met[rim_row, face, pl.ds(2 + side, 1), :]
        weights = jnp.where(lane == 32, rim[:, 0:1], weights)
        extract[face] = jnp.where(lane == 33, rim[:, width - 1 : width], weights)
    table = turned_columns()
    cell_metric[0] = table[0:rows]
    cell_metric[1] = table[16 : 16 + rows]
    corner_metric[0] = table[32:33]
    corner_metric[1] = table[33:34]

    @pl.when(special)
    def _():
        for face in range(faces):
            stack[face] = jnp.broadcast_to(met[rim_row, face, pl.ds(2 + side, 1), :], (levels, width))
        for b in range(blocks):
            span = slice(b * LANES, (b + 1) * LANES)
            rest[span, :] = stack[:, :, span].reshape(LANES, LANES).T
        cut(weight_pieces, rest)
        turn_into(turned, f0[rim_row])
        pack_fan(0)

    pl.semaphore_wait(
        barrier,
        3 + jnp.where(at_first, last, 1) + jnp.where(at_last, last, 1),
    )

    send_columns(0)

    @pl.when(special)
    def _():
        send_fan(0)

    send_rows(0)

    for round_ in range(3):
        source = (f0, f1, f2)[round_]
        target = (f1, f2, out)[round_]
        final = round_ == 2
        apply_interior(source, target, final)
        if final:
            store_copy(0).start()
        if round_ == 0:
            @pl.when(helps)
            def _():
                to_helper().wait_recv()
                for_client().start()

        row_copy(round_, 0).wait_recv()
        row_copy(round_, 1).wait_recv()

        @pl.when(jnp.logical_not(at_first))
        def _():
            add_row(target, 0, 2, lambda face: row_halo[round_, 0, face], final)

        @pl.when(jnp.logical_not(at_last))
        def _():
            add_row(target, rows - 1, 3, lambda face: row_halo[round_, 1, face], final)

        @pl.when(special)
        def _():
            local_seams(round_, source, target, final)

        if not final:
            west, east = take_columns(target)
            part[0] = west
            part[1] = east

            @pl.when(special)
            def _():
                turn_into(turned, target[rim_row])
                cut(part_pieces, turned)

        mirror_copy(round_).wait_recv()
        near = jnp.concatenate(
            [own[round_, 0], own[round_, 1], rows_reversed(mirror[round_, 0]), rows_reversed(mirror[round_, 1])],
            axis=1,
        )
        halo = exact_dot(near, k_halo[: 4 * LANES, :])

        @pl.when(jnp.logical_not(at_first))
        def _():
            pltpu.make_async_copy(piece_in.at[round_, 0], piece_in.at[round_, 0], fan_recv.at[round_, 0]).wait()

        @pl.when(jnp.logical_not(at_last))
        def _():
            pltpu.make_async_copy(piece_in.at[round_, 1], piece_in.at[round_, 1], fan_recv.at[round_, 1]).wait()

        from_south, from_north = piece_in[round_, 0], piece_in[round_, 1]
        far = jnp.concatenate(
            [
                jnp.where(reversed_south, rows_reversed(from_south), from_south),
                jnp.where(reversed_north, rows_reversed(from_north), from_north),
            ],
            axis=1,
        )
        halo = halo + exact_dot(far, k_halo[4 * LANES :, :])
        west = cell_metric[0] * halo[:, :LANES]
        east = cell_metric[1] * halo[:, LANES:]
        fix[0:rows, :] = west
        fix[16 : 16 + rows, :] = east

        if not final:
            @pl.when(special)
            def _():
                all_but_one(piece_all.at[round_], far_recv.at[round_]).wait()
                pack_joined(round_)
                send_fan(round_ + 1)
                flag = codes[pl.ds(2 + side, 1), :] == 1
                low, high = piece_all[round_, 0], piece_all[round_, last]
                west_end = jnp.where(flag, high, low)[0:1]
                east_end = jnp.where(flag, low, high)[rows - 1 : rows]
                part[0, pl.ds(rim_row, 1), :] += corner_metric[0] * west_end
                part[1, pl.ds(rim_row, 1), :] += corner_metric[1] * east_end

            own[round_ + 1, 0] = part[0] + west
            own[round_ + 1, 1] = part[1] + east
            make_far_pieces(round_ + 1)
            send_columns(round_ + 1)

        fix_turned[...] = fix[...].T.reshape(PAD, levels, LANES)
        if final:
            add_columns(target, range(rows), True)

        @pl.when(special)
        def _():
            if final:
                all_but_one(piece_all.at[round_], far_recv.at[round_]).wait()
            join_far(round_)
            for b in range(blocks):
                span = slice(b * LANES, (b + 1) * LANES)
                stack[:, :, span] = rest[span, :].T.reshape(PAD, levels, LANES)
            add_row(target, rim_row, 2 + side, lambda face: stack[face], final)

        if final:
            for index in range(1, 5):
                store_copy(index).start()
        else:
            add_columns(target, (0, rows - 1), False)
            send_rows(round_ + 1)
            add_columns(target, range(1, rows - 1), False)

    for round_ in range(3):
        row_copy(round_, 0).wait_send()
        row_copy(round_, 1).wait_send()
        mirror_copy(round_).wait_send()

        @pl.when(jnp.logical_not(at_first))
        def _():
            far_copy(round_, 0).wait_send()

        @pl.when(jnp.logical_not(at_last))
        def _():
            far_copy(round_, 1).wait_send()

        @pl.when(special)
        def _():
            all_but_one(piece_out.at[round_], fan_send.at[round_]).wait()

    @pl.when(helps)
    def _():
        for_client().wait_send()

    for index in range(5):
        store_copy(index).wait()


def solution(mesh):
    n = mesh.shape["ty"]

    def per_device(fields, damp_four, damp_six, metric, seam_table):
        fields = jnp.transpose(fields, (1, 2, 0, 3))
        metric = jnp.transpose(metric, (1, 2, 0, 3))
        rows, faces, levels, width = fields.shape
        f32, bf16 = jnp.float32, jnp.bfloat16
        vmem, dma = pltpu.VMEM, pltpu.SemaphoreType.DMA
        any_space = pl.BlockSpec(memory_space=pl.ANY)
        in_smem = pl.BlockSpec(memory_space=pltpu.SMEM)
        result = pl.pallas_call(
            functools.partial(kernel, n),
            out_shape=jax.ShapeDtypeStruct(fields.shape, f32),
            in_specs=[any_space, any_space, in_smem, in_smem, in_smem],
            out_specs=any_space,
            scratch_shapes=[
                vmem(fields.shape, f32),
                vmem(fields.shape, f32),
                vmem(fields.shape, f32),
                vmem(fields.shape, f32),
                vmem(metric.shape, f32),
                vmem((3, 2, faces, levels, width), f32),
                vmem((3, 2, rows, LANES), f32),
                vmem((3, 2, rows, LANES), f32),
                vmem((3, 2, rows, LANES), f32),
                vmem((3, n, rows, LANES), f32),
                vmem((3, n, rows, LANES), f32),
                vmem((3, 2, rows, LANES), f32),
                vmem((PAD, levels, width), f32),
                vmem((width, LANES), f32),
                vmem((width, LANES), f32),
                vmem((2, faces, levels, width), f32),
                vmem((n, rows, LANES), f32),
                vmem((n, rows, LANES), f32),
                vmem((rows, LANES), f32),
                vmem((PAD, levels, LANES), f32),
                vmem((2, rows, LANES), f32),
                vmem((2, rows, LANES), f32),
                vmem((2, 1, LANES), f32),
                vmem((LANES, LANES), f32),
                vmem((PAD, levels, LANES), f32),
                vmem((6 * LANES, 2 * LANES), bf16),
                vmem((2 * LANES, 2 * LANES), bf16),
                vmem((8, LANES), jnp.int32),
                vmem((2, levels, LANES), f32),
                dma((2,)),
                dma((5,)),
                dma((3, 2)),
                dma((3, 2)),
                dma((3,)),
                dma((3,)),
                dma((3, 2)),
                dma((3,)),
                dma((3,)),
                dma((3, 2)),
                dma,
                dma,
            ],
            compiler_params=pltpu.CompilerParams(
                collective_id=0, has_side_effects=True, vmem_limit_bytes=60 * 1024 * 1024
            ),
        )(fields, metric, jnp.transpose(seam_table, (2, 1, 0)), damp_four, damp_six)
        return jnp.transpose(result, (2, 0, 1, 3))

    placed = (
        P("member", "ty", None, None),
        P("member"),
        P("member"),
        P(None, "ty", None, None),
        P(),
    )
    return jax.shard_map(
        per_device,
        mesh=mesh,
        in_specs=placed,
        out_specs=P("member", "ty", None, None),
        check_vma=False,
    )
```

```python
import functools

import jax
import jax.numpy as jnp
from jax import lax
from jax.experimental import pallas as pl
from jax.experimental.pallas import tpu as pltpu
from jax.sharding import PartitionSpec as P

MESH = pl.DeviceIdType.MESH
LANES = 128
PAD = 8
SOUTH, EAST, NORTH, WEST = 0, 1, 2, 3


def three_parts(values):
    high = values.astype(jnp.bfloat16).astype(jnp.float32)
    rest = values - high
    middle = rest.astype(jnp.bfloat16).astype(jnp.float32)
    return high, middle, rest - middle


def exact_dot(values, onehot):
    count = values.shape[0]
    short = -count % 8
    if short:
        values = jnp.concatenate([values, jnp.zeros((short, values.shape[1]), jnp.float32)], axis=0)
    whole = count + short
    stacked = jnp.concatenate(three_parts(values), axis=0).astype(jnp.bfloat16)
    product = jnp.dot(stacked, onehot, preferred_element_type=jnp.float32)
    total = product[2 * whole :] + product[whole : 2 * whole] + product[:whole]
    return total[:count]


def exact_left_dot(onehot, values):
    wide = values.shape[1]
    stacked = jnp.concatenate(three_parts(values), axis=1).astype(jnp.bfloat16)
    product = jnp.dot(onehot, stacked, preferred_element_type=jnp.float32)
    return product[:, 2 * wide :] + product[:, wide : 2 * wide] + product[:, :wide]


def rows_reversed(block):
    count = block.shape[0]
    return jnp.concatenate([block[count - 1 - j : count - j] for j in range(count)], axis=0)


def level_eye(shape, code_row, source_code, shift):
    row_lane = lax.broadcasted_iota(jnp.int32, shape, 0)
    column = lax.broadcasted_iota(jnp.int32, shape, 1)
    level = (1 << shift) - 1
    hit = (jnp.bitwise_and(row_lane, level) == jnp.bitwise_and(column, level)) & (
        code_row == lax.shift_right_logical(row_lane, shift) * 4 + source_code
    )
    return jnp.where(hit, 1.0, 0.0).astype(jnp.bfloat16)


def kernel(
    n, fields_hbm, metric_hbm, seam, damp_four, damp_six, out_hbm,
    f0, f1, f2, out, met, row_halo, own, mirror, piece_send, piece_all, piece_out, piece_in,
    stack, turned, rest, picks, part_pieces, weight_pieces, relayed, extract, part, cell_metric, corner_metric,
    fix, fix_turned, k_halo, k_far, codes, damp,
    load_sem, store_sem, row_send, row_recv, mir_send, mir_recv, far_send, far_recv, fan_send, fan_recv,
    relay_send, relay_recv,
):
    rows, faces, levels, width = f0.shape
    shift = levels.bit_length() - 1
    blocks = width // LANES
    me = lax.axis_index("ty")
    last = n - 1
    at_first, at_last = me == 0, me == last
    special = jnp.logical_or(at_first, at_last)
    side = jnp.where(at_last, 1, 0)
    rim_row = side * (rows - 1)
    above, below = lax.rem(me + 1, n), lax.rem(me + last, n)
    opposite = last - me

    reach, stride = 3 * n // 16, n // 4

    def in_lower(device):
        return jnp.logical_and(device >= n // 2 - reach, device < n // 2)

    def in_upper(device):
        return jnp.logical_and(device >= n // 2, device < n // 2 + reach)

    middle_strip = jnp.logical_or(in_lower(me), in_upper(me))
    helper = jnp.where(in_lower(me), me - stride, me + stride)
    helps = jnp.logical_or(in_lower(me + stride), in_upper(me - stride))
    client = jnp.where(in_lower(me + stride), me + stride, me - stride)

    load_fields = pltpu.make_async_copy(fields_hbm, f0, load_sem.at[0])
    load_metric = pltpu.make_async_copy(metric_hbm, met, load_sem.at[1])
    load_fields.start()
    load_metric.start()

    barrier = pltpu.get_barrier_semaphore()

    def greet(device):
        pl.semaphore_signal(barrier, inc=1, device_id={"ty": device}, device_id_type=MESH)

    def spread(i):
        step = (i + 1) // 2
        return lax.rem(me + n // 2 + step * (1 - 2 * lax.rem(i, 2)) + n, n)

    @pl.when(special)
    def _():
        def one(i, _):
            device = spread(i)
            skipped = jnp.logical_or(in_lower(device), in_upper(device))

            @pl.when(jnp.logical_or(at_first, jnp.logical_not(skipped)))
            def _():
                greet(device)

            return 0

        lax.fori_loop(0, last, one, 0)

    @pl.when(jnp.logical_not(at_first))
    def _():
        greet(0)

    @pl.when(jnp.logical_not(at_last))
    def _():
        greet(last)

    @pl.when(helps)
    def _():
        greet(client)

    greet(above)
    greet(below)
    greet(opposite)

    stack[...] = jnp.zeros_like(stack)
    extract[...] = jnp.zeros_like(extract)
    fix[...] = jnp.zeros_like(fix)
    face_of_lane = lax.shift_right_logical(lax.broadcasted_iota(jnp.int32, (1, LANES), 1), shift)

    def lane_row(entry):
        total = jnp.full((1, LANES), -1, jnp.int32)
        for face in range(faces):
            total = jnp.where(face_of_lane == face, entry(face), total)
        return total

    code_of = [lane_row(lambda f, e=e: seam[0, e, f] * 4 + seam[1, e, f]) for e in range(4)]
    flags = [lane_row(lambda f, e=e: seam[2, e, f]) for e in (SOUTH, NORTH)]
    for index, row in enumerate((code_of[SOUTH], code_of[NORTH], flags[0], flags[1])):
        codes[index : index + 1, :] = row
    reversed_south, reversed_north = flags[0] == 1, flags[1] == 1
    square = (LANES, LANES)
    none = jnp.zeros(square, jnp.bfloat16)
    for index, (edge, to_west, to_east) in enumerate(
        ((WEST, 0, 1), (EAST, 1, 0), (WEST, 1, 0), (EAST, 0, 1), (SOUTH, 1, 1), (NORTH, 1, 1))
    ):
        span = slice(index * LANES, (index + 1) * LANES)
        k_halo[span, :LANES] = level_eye(square, code_of[WEST], edge, shift) if to_west else none
        k_halo[span, LANES:] = level_eye(square, code_of[EAST], edge, shift) if to_east else none
    for index, edge in enumerate((WEST, EAST)):
        span = slice(index * LANES, (index + 1) * LANES)
        k_far[span, :LANES] = level_eye(square, code_of[SOUTH], edge, shift)
        k_far[span, LANES:] = level_eye(square, code_of[NORTH], edge, shift)
    level_row = lax.broadcasted_iota(jnp.int32, (levels, LANES), 0)
    for index, source in enumerate((damp_four, damp_six)):
        total = jnp.zeros((levels, LANES), jnp.float32)
        for level in range(levels):
            total = jnp.where(level_row == level, source[level], total)
        damp[index] = total

    lane = lax.broadcasted_iota(jnp.int32, (levels, LANES), 1)
    wide_lane = lax.broadcasted_iota(jnp.int32, (8, width), 1)

    def columns_of(west_tile, east_tile):
        total = jnp.zeros((levels, LANES), jnp.float32)
        for y in range(rows):
            total = jnp.where(lane == y, west_tile(y), total)
            total = jnp.where(lane == 16 + y, east_tile(y), total)
        return total

    def turned_columns():
        return extract[...].reshape(LANES, LANES).T

    def take_columns(source):
        def one(face, _):
            extract[face] = columns_of(
                lambda y: source[y, face, :, 0:LANES][:, 0:1],
                lambda y: source[y, face, :, width - LANES : width][:, LANES - 1 : LANES],
            )
            return 0

        lax.fori_loop(0, faces, one, 0)
        table = turned_columns()
        return table[0:rows], table[16 : 16 + rows]

    def row_copy(round_, way):
        return pltpu.make_async_remote_copy(
            src_ref=(f0, f1, f2)[round_].at[0 if way else rows - 1],
            dst_ref=row_halo.at[round_, way],
            send_sem=row_send.at[round_, way],
            recv_sem=row_recv.at[round_, way],
            device_id={"ty": below if way else above},
            device_id_type=MESH,
        )

    def mirror_copy(round_):
        return pltpu.make_async_remote_copy(
            src_ref=own.at[round_],
            dst_ref=mirror.at[round_],
            send_sem=mir_send.at[round_],
            recv_sem=mir_recv.at[round_],
            device_id={"ty": opposite},
            device_id_type=MESH,
        )

    def far_copy(round_, end):
        return pltpu.make_async_remote_copy(
            src_ref=piece_send.at[round_, end],
            dst_ref=piece_all.at[round_, me],
            send_sem=far_send.at[round_, end],
            recv_sem=far_recv.at[round_],
            device_id={"ty": last if end else 0},
            device_id_type=MESH,
        )

    def to_helper():
        return pltpu.make_async_remote_copy(
            src_ref=piece_send.at[0, 1],
            dst_ref=relayed,
            send_sem=far_send.at[0, 1],
            recv_sem=relay_recv,
            device_id={"ty": helper},
            device_id_type=MESH,
        )

    def for_client():
        return pltpu.make_async_remote_copy(
            src_ref=relayed,
            dst_ref=piece_all.at[0, client],
            send_sem=relay_send,
            recv_sem=far_recv.at[0],
            device_id={"ty": last},
            device_id_type=MESH,
        )

    def fan_copy(round_, device):
        return pltpu.make_async_remote_copy(
            src_ref=piece_out.at[round_, device],
            dst_ref=piece_in.at[round_, side],
            send_sem=fan_send.at[round_],
            recv_sem=fan_recv.at[round_, side],
            device_id={"ty": device},
            device_id_type=MESH,
        )

    def all_but_one(buffer, sem):
        return pltpu.make_async_copy(buffer.at[pl.ds(0, last)], buffer.at[pl.ds(0, last)], sem)

    def make_far_pieces(round_):
        straight = jnp.concatenate([own[round_, 0], own[round_, 1]], axis=1)
        both = jnp.concatenate([straight, rows_reversed(straight)], axis=0)
        chosen = exact_dot(both, k_far[...])
        for end, flag in ((0, reversed_south), (1, reversed_north)):
            span = slice(end * LANES, (end + 1) * LANES)
            piece_send[round_, end] = jnp.where(flag, chosen[rows:, span], chosen[:rows, span])

    def send_columns(round_):
        @pl.when(jnp.logical_not(at_first))
        def _():
            far_copy(round_, 0).start()

        if round_ == 0:
            @pl.when(middle_strip)
            def _():
                to_helper().start()

            @pl.when(jnp.logical_not(jnp.logical_or(middle_strip, at_last)))
            def _():
                far_copy(round_, 1).start()
        else:
            @pl.when(jnp.logical_not(at_last))
            def _():
                far_copy(round_, 1).start()

        mirror_copy(round_).start()

        @pl.when(special)
        def _():
            piece_all[round_, me] = jnp.where(at_last, piece_send[round_, 1], piece_send[round_, 0])

    def send_rows(round_):
        row_copy(round_, 0).start()
        row_copy(round_, 1).start()

    def turn_into(target, planes):
        stack[0:faces] = planes
        for b in range(blocks):
            span = slice(b * LANES, (b + 1) * LANES)
            target[span, :] = stack[:, :, span].reshape(LANES, LANES).T

    def pack_fan(round_):
        flag = codes[pl.ds(2 + side, 1), :] == 1
        for j in range(n):
            here = turned[rows * j : rows * (j + 1), :]
            there = turned[rows * (last - j) : rows * (n - j), :]
            piece_out[round_, j] = jnp.where(flag, there, here)

    def send_fan(round_):
        batch = max(k for k in range(1, 10) if (n - 1) % k == 0)

        def one(i, _):
            for k in range(batch):
                fan_copy(round_, spread(i * batch + k)).start()
            return 0

        lax.fori_loop(0, last // batch, one, 0)
        piece_in[round_, side] = piece_out[round_, me]

    def local_seams(round_, source, target, final):
        up = lax.broadcasted_iota(jnp.int32, square, 0)
        across = lax.broadcasted_iota(jnp.int32, square, 1)
        flip = jnp.where(up + across == LANES - 1, 1.0, 0.0).astype(jnp.bfloat16)
        picks[0] = source[rim_row]
        picks[1] = row_halo[round_, side]
        for face in range(faces):
            joined, edge = seam[0, 2 * side, face], seam[1, 2 * side, face]
            stack[face] = jnp.where(edge == 2 * side, picks[0, joined], 0.0)

        def flipped(b):
            span = slice(b * LANES, (b + 1) * LANES)
            return exact_dot(stack[:, :, span].reshape(LANES, LANES), flip).reshape(PAD, levels, LANES)

        for b in range((blocks + 1) // 2):
            c = blocks - 1 - b
            one, two = flipped(b), flipped(c)
            stack[:, :, c * LANES : (c + 1) * LANES] = one
            stack[:, :, b * LANES : (b + 1) * LANES] = two
        for face in range(faces):
            joined, edge = seam[0, 2 * side, face], seam[1, 2 * side, face]
            value = stack[face] + jnp.where(edge == 2 - 2 * side, picks[1, joined], 0.0)
            value = met[rim_row, face, pl.ds(2 + side, 1), :] * value
            if final:
                value = jnp.concatenate([damp[1]] * blocks, axis=1) * value
            target[rim_row, face] += value

    def join_far(round_):
        flag = codes[pl.ds(2 + side, 1), :] == 1
        for j in range(n):
            span = slice(rows * j, rows * (j + 1))
            rest[span, :] = jnp.where(flag, piece_all[round_, last - j], piece_all[round_, j])

    def pack_joined(round_):
        flag = codes[pl.ds(2 + side, 1), :] == 1
        row = lax.broadcasted_iota(jnp.int32, (rows, LANES), 0)
        for j in range(n // 2):
            k = last - j
            low, high = piece_all[round_, j], piece_all[round_, k]
            one = part_pieces[j] + weight_pieces[j] * jnp.where(flag, high, low)
            two = part_pieces[k] + weight_pieces[k] * jnp.where(flag, low, high)
            if j == 0:
                one = one + jnp.where(row == 0, fix[pl.ds(rim_row, 1), :], 0.0)
                two = two + jnp.where(row == rows - 1, fix[pl.ds(16 + rim_row, 1), :], 0.0)
            piece_out[round_ + 1, j] = jnp.where(flag, two, one)
            piece_out[round_ + 1, k] = jnp.where(flag, one, two)

    def cut(target, source):
        for j in range(n):
            target[j] = source[rows * j : rows * (j + 1), :]

    def apply_interior(source, target, final):
        halves = levels // 8

        def one(step, _):
            face = step // halves
            some = pl.ds(pl.multiple_of(lax.rem(step, halves) * 8, 8), 8)
            cells = [source[y, face, some, :] for y in range(rows)]
            if final:
                four = jnp.concatenate([damp[0, some, :]] * blocks, axis=1)
                six = jnp.concatenate([damp[1, some, :]] * blocks, axis=1)
            for y in range(rows):
                here = cells[y]
                west = jnp.where(wide_lane == 0, 0.0, pltpu.roll(here, 1, 1))
                east = jnp.where(wide_lane == width - 1, 0.0, pltpu.roll(here, width - 1, 1))
                south = cells[y - 1] if y > 0 else jnp.zeros_like(here)
                north = cells[y + 1] if y < rows - 1 else jnp.zeros_like(here)
                value = (
                    met[y, face, 0:1, :] * (west - here)
                    + met[y, face, 1:2, :] * (east - here)
                    + met[y, face, 2:3, :] * (south - here)
                    + met[y, face, 3:4, :] * (north - here)
                )
                if final:
                    value = f0[y, face, some, :] - four * here + six * value
                target[y, face, some, :] = value
            return 0

        lax.fori_loop(0, faces * halves, one, 0)

    def add_row(target, y, weight, halo, final):
        def one(face, _):
            value = met[y, face, pl.ds(weight, 1), :] * halo(face)
            if final:
                value = jnp.concatenate([damp[1]] * blocks, axis=1) * value
            target[y, face] += value
            return 0

        lax.fori_loop(0, faces, one, 0)

    def add_columns(target, which, final):
        def one(face, _):
            table = fix_turned[face]
            if final:
                table = table * damp[1]
            for y in which:
                target[y, face, :, 0:LANES] += jnp.where(lane == 0, table[:, y : y + 1], 0.0)
                target[y, face, :, width - LANES : width] += jnp.where(
                    lane == LANES - 1, table[:, 16 + y : 17 + y], 0.0
                )
            return 0

        lax.fori_loop(0, faces, one, 0)

    middle = pl.ds(LANES, width - 2 * LANES)

    def store_copy(index):
        if index == 0:
            span = (pl.ds(1, rows - 2), slice(None), slice(None), middle)
        elif index < 3:
            span = ((0, rows - 1)[index - 1],)
        else:
            span = (pl.ds(1, rows - 2), slice(None), slice(None), pl.ds((0, width - LANES)[index - 3], LANES))
        return pltpu.make_async_copy(out.at[span], out_hbm.at[span], store_sem.at[index])

    load_fields.wait()
    west, east = take_columns(f0)
    own[0, 0] = west
    own[0, 1] = east
    make_far_pieces(0)
    load_metric.wait()
    for face in range(faces):
        weights = columns_of(
            lambda y: met[y, face, 0:1, 0:LANES][:, 0:1],
            lambda y: met[y, face, 1:2, width - LANES : width][:, LANES - 1 : LANES],
        )
        rim = met[rim_row, face, pl.ds(2 + side, 1), :]
        weights = jnp.where(lane == 32, rim[:, 0:1], weights)
        extract[face] = jnp.where(lane == 33, rim[:, width - 1 : width], weights)
    table = turned_columns()
    cell_metric[0] = table[0:rows]
    cell_metric[1] = table[16 : 16 + rows]
    corner_metric[0] = table[32:33]
    corner_metric[1] = table[33:34]

    @pl.when(special)
    def _():
        for face in range(faces):
            stack[face] = jnp.broadcast_to(met[rim_row, face, pl.ds(2 + side, 1), :], (levels, width))
        for b in range(blocks):
            span = slice(b * LANES, (b + 1) * LANES)
            rest[span, :] = stack[:, :, span].reshape(LANES, LANES).T
        cut(weight_pieces, rest)
        turn_into(turned, f0[rim_row])
        pack_fan(0)

    pl.semaphore_wait(
        barrier,
        3 + jnp.where(at_first, last, 1) + jnp.where(at_last, last, 1),
    )

    send_columns(0)

    @pl.when(special)
    def _():
        send_fan(0)

    send_rows(0)

    for round_ in range(3):
        source = (f0, f1, f2)[round_]
        target = (f1, f2, out)[round_]
        final = round_ == 2
        apply_interior(source, target, final)
        if final:
            store_copy(0).start()
        if round_ == 0:
            @pl.when(helps)
            def _():
                to_helper().wait_recv()
                for_client().start()

        row_copy(round_, 0).wait_recv()
        row_copy(round_, 1).wait_recv()

        @pl.when(jnp.logical_not(at_first))
        def _():
            add_row(target, 0, 2, lambda face: row_halo[round_, 0, face], final)

        @pl.when(jnp.logical_not(at_last))
        def _():
            add_row(target, rows - 1, 3, lambda face: row_halo[round_, 1, face], final)

        @pl.when(special)
        def _():
            local_seams(round_, source, target, final)

        if not final:
            west, east = take_columns(target)
            part[0] = west
            part[1] = east

            @pl.when(special)
            def _():
                turn_into(turned, target[rim_row])
                cut(part_pieces, turned)

        mirror_copy(round_).wait_recv()
        near = jnp.concatenate(
            [own[round_, 0], own[round_, 1], rows_reversed(mirror[round_, 0]), rows_reversed(mirror[round_, 1])],
            axis=1,
        )
        halo = exact_dot(near, k_halo[: 4 * LANES, :])

        @pl.when(jnp.logical_not(at_first))
        def _():
            pltpu.make_async_copy(piece_in.at[round_, 0], piece_in.at[round_, 0], fan_recv.at[round_, 0]).wait()

        @pl.when(jnp.logical_not(at_last))
        def _():
            pltpu.make_async_copy(piece_in.at[round_, 1], piece_in.at[round_, 1], fan_recv.at[round_, 1]).wait()

        from_south, from_north = piece_in[round_, 0], piece_in[round_, 1]
        far = jnp.concatenate(
            [
                jnp.where(reversed_south, rows_reversed(from_south), from_south),
                jnp.where(reversed_north, rows_reversed(from_north), from_north),
            ],
            axis=1,
        )
        halo = halo + exact_dot(far, k_halo[4 * LANES :, :])
        west = cell_metric[0] * halo[:, :LANES]
        east = cell_metric[1] * halo[:, LANES:]
        fix[0:rows, :] = west
        fix[16 : 16 + rows, :] = east

        if not final:
            @pl.when(special)
            def _():
                all_but_one(piece_all.at[round_], far_recv.at[round_]).wait()
                pack_joined(round_)
                send_fan(round_ + 1)
                flag = codes[pl.ds(2 + side, 1), :] == 1
                low, high = piece_all[round_, 0], piece_all[round_, last]
                west_end = jnp.where(flag, high, low)[0:1]
                east_end = jnp.where(flag, low, high)[rows - 1 : rows]
                part[0, pl.ds(rim_row, 1), :] += corner_metric[0] * west_end
                part[1, pl.ds(rim_row, 1), :] += corner_metric[1] * east_end

            own[round_ + 1, 0] = part[0] + west
            own[round_ + 1, 1] = part[1] + east
            make_far_pieces(round_ + 1)
            send_columns(round_ + 1)

        fix_turned[...] = fix[...].T.reshape(PAD, levels, LANES)
        if final:
            add_columns(target, range(rows), True)
            store_copy(3).start()
            store_copy(4).start()

        @pl.when(special)
        def _():
            if final:
                all_but_one(piece_all.at[round_], far_recv.at[round_]).wait()
            join_far(round_)
            for b in range(blocks):
                span = slice(b * LANES, (b + 1) * LANES)
                stack[:, :, span] = rest[span, :].T.reshape(PAD, levels, LANES)
            add_row(target, rim_row, 2 + side, lambda face: stack[face], final)

        if final:
            store_copy(1).start()
            store_copy(2).start()
        else:
            add_columns(target, (0, rows - 1), False)
            send_rows(round_ + 1)
            add_columns(target, range(1, rows - 1), False)

    for round_ in range(3):
        row_copy(round_, 0).wait_send()
        row_copy(round_, 1).wait_send()
        mirror_copy(round_).wait_send()

        @pl.when(jnp.logical_not(at_first))
        def _():
            far_copy(round_, 0).wait_send()

        @pl.when(jnp.logical_not(at_last))
        def _():
            far_copy(round_, 1).wait_send()

        @pl.when(special)
        def _():
            all_but_one(piece_out.at[round_], fan_send.at[round_]).wait()

    @pl.when(helps)
    def _():
        for_client().wait_send()

    for index in range(5):
        store_copy(index).wait()


def solution(mesh):
    n = mesh.shape["ty"]

    def per_device(fields, damp_four, damp_six, metric, seam_table):
        fields = jnp.transpose(fields, (1, 2, 0, 3))
        metric = jnp.transpose(metric, (1, 2, 0, 3))
        rows, faces, levels, width = fields.shape
        f32, bf16 = jnp.float32, jnp.bfloat16
        vmem, dma = pltpu.VMEM, pltpu.SemaphoreType.DMA
        any_space = pl.BlockSpec(memory_space=pl.ANY)
        in_hbm = pl.BlockSpec(memory_space=pltpu.HBM)
        in_smem = pl.BlockSpec(memory_space=pltpu.SMEM)
        operands = (fields, metric, jnp.transpose(seam_table, (2, 1, 0)), damp_four, damp_six)
        result = pl.pallas_call(
            functools.partial(kernel, n),
            out_shape=jax.ShapeDtypeStruct(fields.shape, f32),
            in_specs=[in_hbm, in_hbm, in_smem, in_smem, in_smem],
            out_specs=any_space,
            scratch_shapes=[
                vmem(fields.shape, f32),
                vmem(fields.shape, f32),
                vmem(fields.shape, f32),
                vmem(fields.shape, f32),
                vmem(metric.shape, f32),
                vmem((3, 2, faces, levels, width), f32),
                vmem((3, 2, rows, LANES), f32),
                vmem((3, 2, rows, LANES), f32),
                vmem((3, 2, rows, LANES), f32),
                vmem((3, n, rows, LANES), f32),
                vmem((3, n, rows, LANES), f32),
                vmem((3, 2, rows, LANES), f32),
                vmem((PAD, levels, width), f32),
                vmem((width, LANES), f32),
                vmem((width, LANES), f32),
                vmem((2, faces, levels, width), f32),
                vmem((n, rows, LANES), f32),
                vmem((n, rows, LANES), f32),
                vmem((rows, LANES), f32),
                vmem((PAD, levels, LANES), f32),
                vmem((2, rows, LANES), f32),
                vmem((2, rows, LANES), f32),
                vmem((2, 1, LANES), f32),
                vmem((LANES, LANES), f32),
                vmem((PAD, levels, LANES), f32),
                vmem((6 * LANES, 2 * LANES), bf16),
                vmem((2 * LANES, 2 * LANES), bf16),
                vmem((8, LANES), jnp.int32),
                vmem((2, levels, LANES), f32),
                dma((2,)),
                dma((5,)),
                dma((3, 2)),
                dma((3, 2)),
                dma((3,)),
                dma((3,)),
                dma((3, 2)),
                dma((3,)),
                dma((3,)),
                dma((3, 2)),
                dma,
                dma,
            ],
            compiler_params=pltpu.CompilerParams(
                collective_id=0, has_side_effects=True, vmem_limit_bytes=47 * 1024 * 1024
            ),
        )(*(pltpu.with_memory_space_constraint(x, pltpu.HBM) for x in operands))
        return jnp.transpose(result, (2, 0, 1, 3))

    placed = (
        P("member", "ty", None, None),
        P("member"),
        P("member"),
        P(None, "ty", None, None),
        P(),
    )
    return jax.shard_map(
        per_device,
        mesh=mesh,
        in_specs=placed,
        out_specs=P("member", "ty", None, None),
        check_vma=False,
    )
```
